32 devices in a mesh: row: 4 (over z), col: 8 (over y, x, core).
Axes of the slice: x: 2, y: 2, z: 4, core: 2. Of those that a mesh axis runs over, the one named last changes fastest.
Arguments:
- amplitudes: bfloat16 [2048, 8192], P(('col', 'row')), may hold values from -6 to 6
- integrals: bfloat16 [8192, 8192], P('row', 'col'), may hold values from -0.0625 to 0.0625
- integral_tiles: int32 [64, 64], P('row', 'col'), may hold values from 0 to 1, as said below
- amplitude_tiles: int32 [16, 64], P('col'), may hold values 0 or 1
Outputs:
- ladder: float32 [2048, 8192], P('col', 'row')
The draws below stay inside these ranges and needn't reach their ends.
Inputs may be any that keep to these rules, and one draw needn't show every extreme that they name: `integral_tiles`: tiles of higher ab index are more often nonzero.
All inputs are finite; a program needn't handle non-finite values. No bound on the sum of `amplitude_tiles` on one device may be relied on, other than what follows from the above.
Results may differ from the reference program's by a relative error of at most 0.0003.
Values may be sent and summed in bfloat16 or wider, within the bound.
No kernel may reach another device: no remote copies, remote signals or barrier semaphores. Data moves between devices by JAX's collectives and lax.ppermute only.
A program may use at most 128 MiB of HBM per device.

```python
import jax
import jax.numpy as jnp
from jax import lax

TILE = 128
NT = 64
NP = 8192
OCC = 2048
OTL = 16


def draw_integral_tiles(key, part):
    scores = jax.random.randint(key, (NT, NT), 0, 100)
    limit = 25 + 70 * jnp.arange(NT, dtype=jnp.int32) // NT
    return (scores < limit[:, None]).astype(jnp.int32)


def with_ends(result, own_key, least, high):
    longest = result.shape.index(max(result.shape))
    spots = []
    for shift in (0, 1):
        where = [jax.random.randint(jax.random.fold_in(own_key, axis), (), 0, length) for axis, length in enumerate(result.shape)]
        where[longest] = (where[longest] + shift) % result.shape[longest]
        spots.append(tuple(where))
    return result.at[spots[0]].set(least).at[spots[1]].set(high)


def steps_of(own_key, dims, pieces, smallest, high):
    loudness, own = 1.0, jax.random.fold_in(own_key, 6)
    for position, blocks in pieces:
        heights = jnp.exp(jax.random.uniform(jax.random.fold_in(own, position), (blocks,), jnp.float32, smallest / len(pieces), high / len(pieces)))
        loudness = loudness * jnp.repeat(heights, dims[position] // blocks).reshape([-1 if axis == position else 1 for axis in range(len(dims))])
    return loudness


def gaussian(rng, shape, spread, bound, split=(), held_as=jnp.bfloat16):
    entries = jax.random.normal(rng, shape, jnp.float32) * spread
    if len(split) > 0:
        entries = steps_of(rng, shape, split, -0.22, 0.18) * entries
    return jnp.clip(entries, min=-bound, max=bound).astype(held_as)


def setup_inputs(seed: int = 0) -> dict:
    streams_of = jax.random.split(jax.random.key(seed), 5)
    return {
        "amplitudes": gaussian(streams_of[0], (OCC, NP), 1.0, 6.0, ((0, 32),)),
        "integrals": gaussian(streams_of[1], (NP, NP), NP ** -0.5, 0.0625, ((0, 4), (1, 8))),
        "integral_tiles": draw_integral_tiles(jax.random.fold_in(streams_of[4], 71), 0),
        "amplitude_tiles": with_ends((jax.random.randint(streams_of[3], (OTL, NT), 0, 3) < 2).astype(jnp.int32), jax.random.fold_in(streams_of[3], 1), 0, 1),
    }


def expand(tiles):
    return jnp.repeat(jnp.repeat(tiles, TILE, axis=0), TILE, axis=1)


def reference(amplitudes, integrals, integral_tiles, amplitude_tiles):
    masked_amps = amplitudes * expand(amplitude_tiles).astype(jnp.bfloat16)
    masked_ints = integrals * expand(integral_tiles).astype(jnp.bfloat16)
    return lax.dot_general(masked_amps, masked_ints, (((1,), (1,)), ((), ())), preferred_element_type=jnp.float32)
```

```python
import functools

import jax
import jax.numpy as jnp
import numpy as np
from jax import lax
from jax.experimental import pallas as pl
from jax.experimental.pallas import tpu as pltpu
from jax.sharding import PartitionSpec as P

TILE = 128
LANES = 128
CHUNKS = 2
MIB = 1 << 20


def arrivals(rows):
    order = []
    for z in range(rows):
        mine = []
        for d in range(1, rows):
            if z + d < rows:
                mine.append((d, 1))
            if z - d >= 0:
                mine.append((d, -1))
        order.append(mine)
    return order


def split_amps(info, tiles, amps, *outs, chips, chunks, width):
    chip, tile_row = info[0], info[2]
    rows = amps.shape[0] // chunks
    per = width // TILE
    for d in range(chips):
        there = chip ^ d
        for t in range(per):
            column = pl.multiple_of(there * width + t * TILE, TILE)
            kept = tiles[tile_row, there * per + t] != 0
            block = amps[:, pl.ds(column, TILE)]
            block = jnp.where(kept, block, jnp.zeros_like(block))
            for h in range(chunks):
                outs[h * chips + d][:, t * TILE : (t + 1) * TILE] = block[h * rows : (h + 1) * rows]


def mask_ints(tiles, ints, out):
    step = pl.program_id(0)
    per = ints.shape[0] // TILE
    for r in range(per):
        for t in range(ints.shape[1] // TILE):
            kept = tiles[step * per + r, t] != 0
            block = ints[r * TILE : (r + 1) * TILE, t * TILE : (t + 1) * TILE]
            out[r * TILE : (r + 1) * TILE, t * TILE : (t + 1) * TILE] = jnp.where(kept, block, jnp.zeros_like(block))


def partial_sums(info, *refs, n_pieces, n_choices, which, chips, tn):
    pieces = refs[: n_pieces * n_choices]
    ours, theirs = refs[n_pieces * n_choices : n_pieces * n_choices + 2]
    outs = refs[n_pieces * n_choices + 2 : n_pieces * n_choices + 2 + n_pieces * chips]
    left, total = refs[-2:]
    step = pl.program_id(0)
    rows = pieces[0].shape[0]

    @pl.when(step == 0)
    def _():
        for p in range(n_pieces):
            for c in range(n_choices):
                if n_choices == 1:
                    left[p * rows : (p + 1) * rows] = pieces[p * n_choices + c][...]
                else:

                    @pl.when(info[which] == c)
                    def _():
                        left[p * rows : (p + 1) * rows] = pieces[p * n_choices + c][...]

    half = ours.shape[1]
    core = info[1]
    mine = pl.multiple_of(core * half, half)
    other = pl.multiple_of((1 - core) * half, half)
    dims = (((1,), (1,)), ((), ()))
    sums = lax.dot_general(left[:, pl.ds(mine, half)], ours[...], dims, preferred_element_type=jnp.float32)
    sums += lax.dot_general(left[:, pl.ds(other, half)], theirs[...], dims, preferred_element_type=jnp.float32)
    total[:, pl.ds(pl.multiple_of(step * tn, tn), tn)] = sums

    @pl.when(step == pl.num_programs(0) - 1)
    def _():
        one = rows // chips
        width = total.shape[1]
        for p in range(n_pieces):
            for d in range(chips):
                block = total[p * rows + d * one : p * rows + (d + 1) * one]
                out = outs[p * chips + d]
                if d == 0:
                    out[...] = block
                else:
                    top = jnp.max(jnp.abs(block), axis=1, keepdims=True)
                    power = jnp.ceil(jnp.log2(jnp.maximum(top, 2.0**-100)) + 0.01)
                    out[:, :width] = jnp.round(block * jnp.exp2(14.0 - power) * 1.98).astype(jnp.int32).astype(jnp.int16)
                    out[:, width:] = jnp.broadcast_to(power, (one, LANES)).astype(jnp.int32).astype(jnp.int16)


def add_up(info, *refs, chips):
    own, coded, out = refs[0], refs[1:chips], refs[-1]
    width = own.shape[1]
    total = own[...]
    for ref in coded:
        power = ref[:, width : width + 1].astype(jnp.int32).astype(jnp.float32)
        total += ref[:, :width].astype(jnp.int32).astype(jnp.float32) * (jnp.exp2(power - 14.0) * (1.0 / 1.98))
    out[...] = total


def call(body, name, grid, in_specs, out_specs, out_shape, scalars, args, scratch=(), flops=0, moved=0, aliases=None):
    return pl.pallas_call(
        body,
        out_shape=out_shape,
        grid_spec=pltpu.PrefetchScalarGridSpec(
            num_scalar_prefetch=len(scalars), grid=grid, in_specs=in_specs, out_specs=out_specs, scratch_shapes=list(scratch)
        ),
        compiler_params=pltpu.CompilerParams(vmem_limit_bytes=40 * MIB),
        cost_estimate=pl.CostEstimate(flops=flops, bytes_accessed=moved, transcendentals=0),
        input_output_aliases=aliases or {},
        name=name,
    )(*scalars, *args)


def whole(shape):
    return pl.BlockSpec(shape, lambda *_: (0,) * len(shape))


def on_device(n_row, n_col, amplitudes, integrals, integral_tiles, amplitude_tiles):
    chips, chunks = n_col // 2, CHUNKS
    m, cds = amplitudes.shape
    width = cds // chips
    rows = m // chunks
    nab, half = integrals.shape

    order = arrivals(n_row)
    choices, table = [], []
    for j in range(n_row - 1):
        choices.append(sorted({order[z][j] for z in range(n_row)}))
    for z in range(n_row):
        sources = [z] + [z + d * side for d, side in order[z]]
        picks = [0] + [choices[j].index(order[z][j]) for j in range(n_row - 1)]
        for c in range(n_col):
            table.append([c // 2, c % 2, z * m // TILE, *picks, *sources])
    table = np.array(table, np.int32)
    here = lax.axis_index("row") * n_col + lax.axis_index("col")
    info = lax.dynamic_index_in_dim(jnp.asarray(table), here, 0, keepdims=False)
    pick_at, source_at = 3, 3 + n_row

    def over(d):
        return [(i, i ^ (2 * d)) for i in range(n_col)]

    parts = call(
        functools.partial(split_amps, chips=chips, chunks=chunks, width=width),
        "split_amps",
        (1,),
        [whole(amplitudes.shape)],
        [whole((rows, width))] * (chips * chunks),
        [jax.ShapeDtypeStruct((rows, width), jnp.bfloat16)] * (chips * chunks),
        (info, amplitude_tiles),
        (amplitudes,),
        moved=4 * m * cds,
    )
    pieces = []
    for h in range(chunks):
        got = [parts[h * chips]]
        for d in range(1, chips):
            got.append(lax.ppermute(parts[h * chips + d], "col", over(d)))
        pieces.append(jnp.concatenate(got, axis=0))

    tall = min(512, nab)
    ours = call(
        mask_ints,
        "mask_ints",
        (nab // tall,),
        [pl.BlockSpec((tall, half), lambda i, *_: (i, 0))],
        pl.BlockSpec((tall, half), lambda i, *_: (i, 0)),
        jax.ShapeDtypeStruct(integrals.shape, jnp.bfloat16),
        (integral_tiles,),
        (integrals,),
        moved=4 * nab * half,
    )
    theirs = lax.ppermute(ours, "col", [(i, i ^ 1) for i in range(n_col)])

    came = []
    for h in range(chunks):
        held = {(0, 1): pieces[h], (0, -1): pieces[h]}
        for d in range(1, n_row):
            down = [(i + 1, i) for i in range(n_row - 1) if i + d < n_row]
            up = [(i, i + 1) for i in range(n_row - 1) if i - d + 1 >= 0]
            held[(d, 1)] = lax.ppermute(held[(d - 1, 1)], "row", down)
            held[(d, -1)] = lax.ppermute(held[(d - 1, -1)], "row", up)
        came.append(held)

    tn = min(512, nab)
    result = None
    for j in range(n_row):
        wanted = [(0, 1)] if j == 0 else choices[j - 1]
        last = j == n_row - 1
        groups = [[h] for h in range(chunks)] if last else [list(range(chunks))]
        for group in groups:
            operands = [came[h][w] for h in group for w in wanted]
            tall = chips * rows
            outs = call(
                functools.partial(
                    partial_sums, n_pieces=len(group), n_choices=len(wanted), which=pick_at + j, chips=chips, tn=tn
                ),
                "partial_sums",
                (nab // tn,),
                [whole((tall, width))] * len(operands) + [pl.BlockSpec((tn, half), lambda i, *_: (i, 0))] * 2,
                ([whole((rows, nab))] + [whole((rows, nab + LANES))] * (chips - 1)) * len(group),
                (
                    [jax.ShapeDtypeStruct((rows, nab), jnp.float32)]
                    + [jax.ShapeDtypeStruct((rows, nab + LANES), jnp.int16)] * (chips - 1)
                )
                * len(group),
                (info,),
                (*operands, ours, theirs),
                scratch=[
                    pltpu.VMEM((len(group) * tall, width), jnp.bfloat16),
                    pltpu.VMEM((len(group) * tall, nab), jnp.float32),
                ],
                flops=2 * len(group) * tall * width * nab,
                moved=4 * nab * half,
            )
            for p, h in enumerate(group):
                own = outs[p * chips]
                coded = [lax.ppermute(outs[p * chips + d], "col", over(d)) for d in range(1, chips)]
                place = lambda i, info, j=j, h=h: (info[source_at + j] * chunks + h, 0)
                body = functools.partial(add_up, chips=chips)
                specs = [whole(x.shape) for x in (own, *coded)]
                args = (own, *coded)
                aliases = {}
                if result is not None:
                    body = functools.partial(lambda f, info, base, *refs: f(info, *refs), body)
                    specs = [pl.BlockSpec(memory_space=pl.ANY)] + specs
                    args = (result, *args)
                    aliases = {1: 0}
                result = call(
                    body,
                    "add_up",
                    (1,),
                    specs,
                    pl.BlockSpec((rows, nab), place),
                    jax.ShapeDtypeStruct((n_row * m, nab), jnp.float32),
                    (info,),
                    args,
                    aliases=aliases,
                    moved=16 * rows * nab,
                )
    return result


def solution(mesh):
    return jax.shard_map(
        functools.partial(on_device, mesh.shape["row"], mesh.shape["col"]),
        mesh=mesh,
        in_specs=(P(("col", "row"), None), P("row", "col"), P("row", "col"), P("col", None)),
        out_specs=P("col", "row"),
        check_vma=False,
    )
```

```python
import functools

import jax
import jax.numpy as jnp
import numpy as np
from jax import lax
from jax.experimental import pallas as pl
from jax.experimental.pallas import tpu as pltpu
from jax.sharding import PartitionSpec as P

TILE = 128
LANES = 128
CHUNKS = 2
MIB = 1 << 20


def row_plan(rows, chunks):
    moves, slots, steps = {}, [], []
    everything = tuple(range(chunks))
    if rows == 4 and chunks == 2:
        middle, outward = [(1, 2), (2, 1)], [(1, 0), (2, 3)]
        moves = {
            "pair": ("own", [(0, 1), (1, 0), (2, 3), (3, 2)]),
            "cross": ("own", middle),
            "far": ("cross", outward),
            "cross2": ("pair", middle),
            "far2": ("cross2", outward),
        }
        slots = [
            (["pair"], [0, 0, 0, 0], [1, 0, 3, 2]),
            (["far", "cross"], [0, 1, 1, 0], [2, 2, 1, 1]),
            (["far2", "cross2"], [0, 1, 1, 0], [3, 3, 0, 0]),
        ]
        steps = [
            ("move", "cross", 0, ()),
            ("move", "pair", 0, ()),
            ("multiply", 0, everything, ()),
            ("move", "cross", 1, ()),
            ("move", "pair", 1, (("own", 0), )),
            ("move", "far", 0, ()),
            ("multiply", 1, everything, (("far", 0), )),
            ("move", "cross2", 0, (("cross", 1), )),
            ("move", "far", 1, (("own", 1), )),
            ("add", 0, (everything,)),
            ("move", "cross2", 1, ()),
            ("move", "far2", 0, (("own", 0), )),
            ("multiply", 2, everything, ()),
            ("add", 1, (everything,)),
            ("move", "far2", 1, (("own", 2), ("result",), )),
            ("multiply", 3, everything, ()),
            ("add", 2, (everything,)),
            ("add", 3, (everything,)),
        ]
        return moves, slots, steps
    order = [[] for _ in range(rows)]
    for d in range(1, rows):
        low, high = f"low{d}", f"high{d}"
        moves[high] = (f"high{d - 1}" if d > 1 else "own", [(i + 1, i) for i in range(rows - d)])
        moves[low] = (f"low{d - 1}" if d > 1 else "own", [(i, i + 1) for i in range(d - 1, rows - 1)])
        for z in range(rows):
            order[z] += [(high, z + d)] * (z + d < rows) + [(low, z - d)] * (z >= d)
        steps += [("move", name, h, ()) for name in (high, low) for h in everything]
    for j in range(rows - 1):
        names = sorted({order[z][j][0] for z in range(rows)})
        slots.append((names, [names.index(order[z][j][0]) for z in range(rows)], [order[z][j][1] for z in range(rows)]))
    steps += [("multiply", j, everything, ()) for j in range(rows)] + [("add", j, (everything,)) for j in range(rows)]
    return moves, slots, steps


def split_amps(tiles, amps, *outs, chips, starts, width):
    chip, tile_row = lax.axis_index("col") // 2, lax.axis_index("row") * amps.shape[0] // TILE
    per = width // TILE
    for d in range(chips):
        there = chip ^ d
        for t in range(per):
            column = pl.multiple_of(there * width + t * TILE, TILE)
            kept = tiles[tile_row, there * per + t] != 0
            block = amps[:, pl.ds(column, TILE)]
            block = jnp.where(kept, block, jnp.zeros_like(block))
            for h in range(len(starts) - 1):
                outs[h * chips + d][:, t * TILE : (t + 1) * TILE] = block[starts[h] : starts[h + 1]]


def masked(block, tiles, first):
    rows = []
    for r in range(block.shape[0] // TILE):
        row = []
        for t in range(block.shape[1] // TILE):
            tile = block[r * TILE : (r + 1) * TILE, t * TILE : (t + 1) * TILE]
            row.append(jnp.where(tiles[first + r, t] != 0, tile, jnp.zeros_like(tile)))
        rows.append(jnp.concatenate(row, axis=1))
    return jnp.concatenate(rows, axis=0)


def first_sums(info, our_tiles, their_tiles, piece, *refs, **kw):
    n = kw["n_pieces"] - 1
    more, (ours, theirs), outs = refs[:n], refs[n : n + 2], refs[n + 2 :]
    our_kept, their_kept = outs[-4:-2]
    first = pl.program_id(0) * (ours.shape[0] // TILE)
    our_kept[...] = masked(ours[...], our_tiles, first)
    their_kept[...] = masked(theirs[...], their_tiles, first)
    partial_sums(info, piece, *more, our_kept, their_kept, *outs[:-4], *outs[-2:], **kw)


def partial_sums(info, *refs, n_pieces, n_choices, which, chips, tn):
    pieces = refs[: n_pieces * n_choices]
    ours, theirs = refs[n_pieces * n_choices : n_pieces * n_choices + 2]
    outs = refs[n_pieces * n_choices + 2 : -2]
    left, total = refs[-2:]
    step = pl.program_id(0)
    rows = [pieces[p * n_choices].shape[0] for p in range(n_pieces)]
    at = [sum(rows[:p]) for p in range(n_pieces)]

    @pl.when(step == 0)
    def _():
        for p in range(n_pieces):
            for c in range(n_choices):

                @pl.when((info[which] == c) if n_choices > 1 else True)
                def _():
                    left[at[p] : at[p] + rows[p]] = pieces[p * n_choices + c][...]

    half = ours.shape[1]
    core = info[1]
    mine = pl.multiple_of(core * half, half)
    other = pl.multiple_of((1 - core) * half, half)
    dims = (((1,), (1,)), ((), ()))
    sums = lax.dot_general(left[:, pl.ds(mine, half)], ours[...], dims, preferred_element_type=jnp.float32)
    sums += lax.dot_general(left[:, pl.ds(other, half)], theirs[...], dims, preferred_element_type=jnp.float32)
    total[:, pl.ds(pl.multiple_of(step * tn, tn), tn)] = sums

    @pl.when(step == pl.num_programs(0) - 1)
    def _():
        for p in range(n_pieces):
            one = rows[p] // chips
            there = slice(at[p] // chips, at[p] // chips + one)
            for d in range(chips):
                block = total[at[p] + d * one : at[p] + (d + 1) * one]
                if d == 0:
                    outs[0][there] = block
                else:
                    encode(block, outs[d].at[there])


def encode(block, out):
    width = block.shape[1]
    top = jnp.max(jnp.abs(block), axis=1, keepdims=True)
    power = jnp.ceil(jnp.log2(jnp.maximum(top, 2.0**-100)) + 0.01)
    out[:, :width] = jnp.round(block * (jnp.exp2(14.0 - power) * 1.98)).astype(jnp.int32).astype(jnp.int16)
    out[:, width:] = jnp.broadcast_to(power, (block.shape[0], LANES)).astype(jnp.int32).astype(jnp.int16)


def decode(coded, width):
    power = coded[:, width : width + 1].astype(jnp.int32).astype(jnp.float32)
    return coded[:, :width].astype(jnp.int32).astype(jnp.float32) * (jnp.exp2(power - 14.0) * (1.0 / 1.98))


def add_up(info, *refs, chips):
    sets, out, at = refs[:-1], refs[-1], 0
    for g in range(0, len(sets), chips):
        total = sets[g][...]
        for d in range(1, chips):
            total += decode(sets[g + d][...], total.shape[1])
        out[at : at + total.shape[0]] = total
        at += total.shape[0]


def call(body, name, grid, in_specs, out_specs, out_shape, scalars, args, scratch=(), flops=0, moved=0, aliases=None):
    return pl.pallas_call(
        body,
        out_shape=out_shape,
        grid_spec=pltpu.PrefetchScalarGridSpec(
            num_scalar_prefetch=len(scalars), grid=grid, in_specs=in_specs, out_specs=out_specs, scratch_shapes=list(scratch)
        ),
        compiler_params=pltpu.CompilerParams(vmem_limit_bytes=24 * MIB),
        cost_estimate=pl.CostEstimate(flops=flops, bytes_accessed=0, transcendentals=0),
        input_output_aliases=aliases or {},
        name=name,
    )(*scalars, *args)


def whole(shape):
    return pl.BlockSpec(shape, lambda *_: (0,) * len(shape))


def on_device(n_row, n_col, amplitudes, integrals, integral_tiles, amplitude_tiles):
    chips, chunks = n_col // 2, CHUNKS
    m, cds = amplitudes.shape
    width = cds // chips
    starts = [0, 3 * m // 4, m]
    rows_of = [b - a for a, b in zip(starts, starts[1:])]
    nab, half = integrals.shape

    moves, slots, steps = row_plan(n_row, chunks)
    table = []
    for z in range(n_row):
        picks = [0] + [slot[1][z] for slot in slots]
        sources = [z] + [slot[2][z] for slot in slots]
        for c in range(n_col):
            table.append([c // 2, c % 2, z * m // TILE, *picks, *sources])
    table = np.array(table, np.int32)
    here = lax.axis_index("row") * n_col + lax.axis_index("col")
    info = lax.dynamic_index_in_dim(jnp.asarray(table), here, 0, keepdims=False)
    pick_at, source_at = 3, 3 + n_row

    def over(d):
        return [(i, i ^ (2 * d)) for i in range(n_col)]

    swap = [(i, i ^ 1) for i in range(n_col)]
    theirs = lax.ppermute(integrals, "col", swap)
    their_tiles = lax.ppermute(integral_tiles, "col", swap)
    kept = []

    parts = call(
        functools.partial(split_amps, chips=chips, starts=starts, width=width),
        "split_amps",
        (1,),
        [whole(amplitudes.shape)],
        [whole((rows, width)) for rows in rows_of for _ in range(chips)],
        [jax.ShapeDtypeStruct((rows, width), jnp.bfloat16) for rows in rows_of for _ in range(chips)],
        (amplitude_tiles,),
        (amplitudes,),
        moved=4 * m * cds,
    )
    pieces = []
    for h in range(chunks):
        got = [parts[h * chips]]
        for d in range(1, chips):
            part = parts[h * chips + d]
            got.append(lax.ppermute(after(part, their_tiles) if h else part, "col", over(d)))
        pieces.append(jnp.concatenate(got, axis=0))

    tn = min(512, nab)

    def multiply(j, operands, group):
        wanted = ["own"] if j == 0 else slots[j - 1][0]
        many = sum(rows_of[h] for h in group)
        block = pl.BlockSpec((tn, half), lambda i, *_: (i, 0))
        out = [((many, nab), jnp.float32)] + [((many, nab + LANES), jnp.int16)] * (chips - 1)
        outs = call(
            functools.partial(
                partial_sums if j else first_sums,
                n_pieces=len(group),
                n_choices=len(wanted),
                which=pick_at + j,
                chips=chips,
                tn=tn,
            ),
            "partial_sums" if j else "first_sums",
            (nab // tn,),
            [whole(x.shape) for x in operands] + [block] * 2,
            [whole(shape) for shape, _ in out] + ([] if j else [block] * 2),
            [jax.ShapeDtypeStruct(*x) for x in out] + ([] if j else [jax.ShapeDtypeStruct((nab, half), jnp.bfloat16)] * 2),
            (info,) if j else (info, integral_tiles, their_tiles),
            (*operands, *(kept if j else (pltpu.with_memory_space_constraint(integrals, pltpu.HBM), theirs))),
            scratch=[
                pltpu.VMEM((chips * many, width), jnp.bfloat16),
                pltpu.VMEM((chips * many, nab), jnp.float32),
            ],

        )
        if not j:
            kept.extend(outs[-2:])
        return [outs[0]] + [lax.ppermute(outs[d], "col", over(d)) for d in range(1, chips)]

    def gather(result, j, sums):
        def place(i, info):
            return (info[source_at + j], 0)

        body = functools.partial(add_up, chips=chips)
        specs = [whole(x.shape) for x in sums]
        args, aliases = tuple(sums), {}
        if result is not None:
            body = functools.partial(lambda f, info, base, *refs: f(info, *refs), body)
            specs = [pl.BlockSpec(memory_space=pl.ANY)] + specs
            args, aliases = (result, *args), {1: 0}
        return call(
            body,
            "add_up",
            (1,),
            specs,
            pl.BlockSpec((m, nab), place),
            jax.ShapeDtypeStruct((n_row * m, nab), jnp.float32),
            (info,),
            args,
            aliases=aliases,
            moved=16 * m * nab,
        )

    held = [{"own": pieces[h]} for h in range(chunks)]
    sums, result = {}, None

    def tied(value, ties):
        nonlocal result
        for kind, *at in ties:
            if kind == "result":
                value, result = lax.optimization_barrier((value, result))
            elif kind == "own":
                value = after(value, sums[at[0], tuple(range(chunks))][0])
            elif kind == "others":
                value = after(value, *sums[at[0], tuple(range(chunks))][1:])
            else:
                value = after(value, held[at[0]][kind])
        return value

    for kind, *step in steps:
        if kind == "move":
            name, h, ties = step
            sent, pairs = moves[name]
            held[h][name] = lax.ppermute(tied(held[h][sent], ties), "row", pairs)
        elif kind == "multiply":
            j, group, ties = step
            operands = [held[h][w] for h in group for w in (slots[j - 1][0] if j else ["own"])]
            operands[0] = tied(operands[0], ties)
            sums[j, group] = multiply(j, operands, group)
        else:
            j, groups = step
            result = gather(result, j, [x for group in groups for x in sums[j, group]])
    return result


def after(value, *others):
    return lax.optimization_barrier((value, *others))[0]


def solution(mesh):
    return jax.shard_map(
        functools.partial(on_device, mesh.shape["row"], mesh.shape["col"]),
        mesh=mesh,
        in_specs=(P(("col", "row"), None), P("row", "col"), P("row", "col"), P("col", None)),
        out_specs=P("col", "row"),
        check_vma=False,
    )
```

```python
import functools

import jax
import jax.numpy as jnp
import numpy as np
from jax import lax
from jax.experimental import pallas as pl
from jax.experimental.pallas import tpu as pltpu
from jax.sharding import PartitionSpec as P

TILE = 128
LANES = 128
CHUNKS = 2
MIB = 1 << 20


def row_plan(rows, chunks):
    moves, slots, steps = {}, [], []
    everything = tuple(range(chunks))
    if rows == 4 and chunks == 2:
        middle, outward = [(1, 2), (2, 1)], [(1, 0), (2, 3)]
        moves = {
            "pair": ("own", [(0, 1), (1, 0), (2, 3), (3, 2)]),
            "cross": ("own", middle),
            "far": ("cross", outward),
            "cross2": ("pair", middle),
            "far2": ("cross2", outward),
        }
        slots = [
            (["pair"], [0, 0, 0, 0], [1, 0, 3, 2]),
            (["far", "cross"], [0, 1, 1, 0], [2, 2, 1, 1]),
            (["far2", "cross2"], [0, 1, 1, 0], [3, 3, 0, 0]),
        ]
        steps = [
            ("move", "cross", 0, ()),
            ("move", "pair", 0, ()),
            ("multiply", 0, everything, ()),
            ("move", "cross", 1, (("own", 0),)),
            ("move", "pair", 1, (("own", 0),)),
            ("move", "far", 0, ()),
            ("multiply", 1, everything, (("far", 0),)),
            ("move", "cross2", 0, (("cross", 1),)),
            ("move", "far", 1, (("own", 1),)),
            ("move", "cross2", 1, (("cross2", 0),)),
            ("move", "far2", 0, (("own", 0),)),
            ("multiply", 2, everything, ()),
            ("move", "far2", 1, (("own", 2), ("others", 0), ("others", 1))),
            ("multiply", 3, everything, ()),
            ("add", 0, (everything,)),
            ("add", 1, (everything,)),
            ("add", 2, (everything,)),
            ("add", 3, (everything,)),
        ]
        return moves, slots, steps
    order = [[] for _ in range(rows)]
    for d in range(1, rows):
        low, high = f"low{d}", f"high{d}"
        moves[high] = (f"high{d - 1}" if d > 1 else "own", [(i + 1, i) for i in range(rows - d)])
        moves[low] = (f"low{d - 1}" if d > 1 else "own", [(i, i + 1) for i in range(d - 1, rows - 1)])
        for z in range(rows):
            order[z] += [(high, z + d)] * (z + d < rows) + [(low, z - d)] * (z >= d)
        steps += [("move", name, h, ()) for name in (high, low) for h in everything]
    for j in range(rows - 1):
        names = sorted({order[z][j][0] for z in range(rows)})
        slots.append((names, [names.index(order[z][j][0]) for z in range(rows)], [order[z][j][1] for z in range(rows)]))
    steps += [("multiply", j, everything, ()) for j in range(rows)] + [("add", j, (everything,)) for j in range(rows)]
    return moves, slots, steps


def split_amps(tiles, amps, *outs, chips, starts, width):
    chip, tile_row = lax.axis_index("col") // 2, lax.axis_index("row") * amps.shape[0] // TILE
    per = width // TILE
    for d in range(chips):
        there = chip ^ d
        for t in range(per):
            column = pl.multiple_of(there * width + t * TILE, TILE)
            kept = tiles[tile_row, there * per + t] != 0
            block = amps[:, pl.ds(column, TILE)]
            block = jnp.where(kept, block, jnp.zeros_like(block))
            for h in range(len(starts) - 1):
                outs[h * chips + d][:, t * TILE : (t + 1) * TILE] = block[starts[h] : starts[h + 1]]


def masked(block, tiles, first):
    rows = []
    for r in range(block.shape[0] // TILE):
        row = []
        for t in range(block.shape[1] // TILE):
            tile = block[r * TILE : (r + 1) * TILE, t * TILE : (t + 1) * TILE]
            row.append(jnp.where(tiles[first + r, t] != 0, tile, jnp.zeros_like(tile)))
        rows.append(jnp.concatenate(row, axis=1))
    return jnp.concatenate(rows, axis=0)


def first_sums(info, our_tiles, their_tiles, piece, *refs, **kw):
    n = kw["n_pieces"] - 1
    more, (ours, theirs), outs = refs[:n], refs[n : n + 2], refs[n + 2 :]
    our_kept, their_kept = outs[-4:-2]
    first = pl.program_id(0) * (ours.shape[0] // TILE)
    our_kept[...] = masked(ours[...], our_tiles, first)
    their_kept[...] = masked(theirs[...], their_tiles, first)
    partial_sums(info, piece, *more, our_kept, their_kept, *outs[:-4], *outs[-2:], **kw)


def partial_sums(info, *refs, n_pieces, n_choices, which, chips, tn):
    pieces = refs[: n_pieces * n_choices]
    ours, theirs = refs[n_pieces * n_choices : n_pieces * n_choices + 2]
    outs = refs[n_pieces * n_choices + 2 : -2]
    left, total = refs[-2:]
    step = pl.program_id(0)
    rows = [pieces[p * n_choices].shape[0] for p in range(n_pieces)]
    at = [sum(rows[:p]) for p in range(n_pieces)]

    @pl.when(step == 0)
    def _():
        for p in range(n_pieces):
            for c in range(n_choices):

                @pl.when((info[which] == c) if n_choices > 1 else True)
                def _():
                    left[at[p] : at[p] + rows[p]] = pieces[p * n_choices + c][...]

    half = ours.shape[1]
    core = info[1]
    mine = pl.multiple_of(core * half, half)
    other = pl.multiple_of((1 - core) * half, half)
    dims = (((1,), (1,)), ((), ()))
    sums = lax.dot_general(left[:, pl.ds(mine, half)], ours[...], dims, preferred_element_type=jnp.float32)
    sums += lax.dot_general(left[:, pl.ds(other, half)], theirs[...], dims, preferred_element_type=jnp.float32)
    total[:, pl.ds(pl.multiple_of(step * tn, tn), tn)] = sums

    @pl.when(step == pl.num_programs(0) - 1)
    def _():
        for p in range(n_pieces):
            one = rows[p] // chips
            there = slice(at[p] // chips, at[p] // chips + one)
            for d in range(chips):
                block = total[at[p] + d * one : at[p] + (d + 1) * one]
                if d == 0:
                    outs[0][there] = block
                else:
                    encode(block, outs[d].at[there])


def encode(block, out):
    width = block.shape[1]
    top = jnp.max(jnp.abs(block), axis=1, keepdims=True)
    power = jnp.ceil(jnp.log2(jnp.maximum(top, 2.0**-100)) + 0.01)
    out[:, :width] = jnp.round(block * (jnp.exp2(14.0 - power) * 1.98)).astype(jnp.int32).astype(jnp.int16)
    out[:, width:] = jnp.broadcast_to(power, (block.shape[0], LANES)).astype(jnp.int32).astype(jnp.int16)


def decode(coded, width):
    power = coded[:, width : width + 1].astype(jnp.int32).astype(jnp.float32)
    return coded[:, :width].astype(jnp.int32).astype(jnp.float32) * (jnp.exp2(power - 14.0) * (1.0 / 1.98))


def add_up(info, *refs, chips):
    sets, out, at = refs[:-1], refs[-1], 0
    for g in range(0, len(sets), chips):
        total = sets[g][...]
        for d in range(1, chips):
            total += decode(sets[g + d][...], total.shape[1])
        out[at : at + total.shape[0]] = total
        at += total.shape[0]


def call(body, name, grid, in_specs, out_specs, out_shape, scalars, args, scratch=(), flops=0, moved=0, aliases=None):
    return pl.pallas_call(
        body,
        out_shape=out_shape,
        grid_spec=pltpu.PrefetchScalarGridSpec(
            num_scalar_prefetch=len(scalars), grid=grid, in_specs=in_specs, out_specs=out_specs, scratch_shapes=list(scratch)
        ),
        compiler_params=pltpu.CompilerParams(vmem_limit_bytes=24 * MIB),
        cost_estimate=pl.CostEstimate(flops=flops, bytes_accessed=0, transcendentals=0),
        input_output_aliases=aliases or {},
        name=name,
    )(*scalars, *args)


def whole(shape):
    return pl.BlockSpec(shape, lambda *_: (0,) * len(shape))


def on_device(n_row, n_col, amplitudes, integrals, integral_tiles, amplitude_tiles):
    chips, chunks = n_col // 2, CHUNKS
    m, cds = amplitudes.shape
    width = cds // chips
    starts = [0, 3 * m // 4, m]
    rows_of = [b - a for a, b in zip(starts, starts[1:])]
    nab, half = integrals.shape

    moves, slots, steps = row_plan(n_row, chunks)
    table = []
    for z in range(n_row):
        picks = [0] + [slot[1][z] for slot in slots]
        sources = [z] + [slot[2][z] for slot in slots]
        for c in range(n_col):
            table.append([c // 2, c % 2, z * m // TILE, *picks, *sources])
    table = np.array(table, np.int32)
    here = lax.axis_index("row") * n_col + lax.axis_index("col")
    info = lax.dynamic_index_in_dim(jnp.asarray(table), here, 0, keepdims=False)
    pick_at, source_at = 3, 3 + n_row

    def over(d):
        return [(i, i ^ (2 * d)) for i in range(n_col)]

    swap = [(i, i ^ 1) for i in range(n_col)]
    theirs = lax.ppermute(integrals, "col", swap)
    their_tiles = lax.ppermute(integral_tiles, "col", swap)
    kept = []

    parts = call(
        functools.partial(split_amps, chips=chips, starts=starts, width=width),
        "split_amps",
        (1,),
        [whole(amplitudes.shape)],
        [whole((rows, width)) for rows in rows_of for _ in range(chips)],
        [jax.ShapeDtypeStruct((rows, width), jnp.bfloat16) for rows in rows_of for _ in range(chips)],
        (amplitude_tiles,),
        (amplitudes,),
        moved=4 * m * cds,
    )
    pieces = []
    for h in range(chunks):
        got = [parts[h * chips]]
        for d in range(1, chips):
            part = parts[h * chips + d]
            got.append(lax.ppermute(after(part, their_tiles) if h else part, "col", over(d)))
        pieces.append(jnp.concatenate(got, axis=0))

    tn = min(512, nab)

    def multiply(j, operands, group):
        wanted = ["own"] if j == 0 else slots[j - 1][0]
        many = sum(rows_of[h] for h in group)
        block = pl.BlockSpec((tn, half), lambda i, *_: (i, 0))
        out = [((many, nab), jnp.float32)] + [((many, nab + LANES), jnp.int16)] * (chips - 1)
        outs = call(
            functools.partial(
                partial_sums if j else first_sums,
                n_pieces=len(group),
                n_choices=len(wanted),
                which=pick_at + j,
                chips=chips,
                tn=tn,
            ),
            "partial_sums" if j else "first_sums",
            (nab // tn,),
            [whole(x.shape) for x in operands] + [block] * 2,
            [whole(shape) for shape, _ in out] + ([] if j else [block] * 2),
            [jax.ShapeDtypeStruct(*x) for x in out] + ([] if j else [jax.ShapeDtypeStruct((nab, half), jnp.bfloat16)] * 2),
            (info,) if j else (info, integral_tiles, their_tiles),
            (*operands, *(kept if j else (pltpu.with_memory_space_constraint(integrals, pltpu.HBM), theirs))),
            scratch=[
                pltpu.VMEM((chips * many, width), jnp.bfloat16),
                pltpu.VMEM((chips * many, nab), jnp.float32),
            ],
        )
        if not j:
            kept.extend(outs[-2:])
        return [outs[0]] + [lax.ppermute(outs[d], "col", over(d)) for d in range(1, chips)]

    def gather(result, j, sums):
        def place(i, info):
            return (info[source_at + j], 0)

        body = functools.partial(add_up, chips=chips)
        specs = [whole(x.shape) for x in sums]
        args, aliases = tuple(sums), {}
        if result is not None:
            body = functools.partial(lambda f, info, base, *refs: f(info, *refs), body)
            specs = [pl.BlockSpec(memory_space=pl.ANY)] + specs
            args, aliases = (result, *args), {1: 0}
        return call(
            body,
            "add_up",
            (1,),
            specs,
            pl.BlockSpec((m, nab), place),
            jax.ShapeDtypeStruct((n_row * m, nab), jnp.float32),
            (info,),
            args,
            aliases=aliases,
            moved=16 * m * nab,
        )

    held = [{"own": pieces[h]} for h in range(chunks)]
    sums, result = {}, None

    def tied(value, ties):
        nonlocal result
        for kind, *at in ties:
            if kind == "result":
                value, result = lax.optimization_barrier((value, result))
            elif kind == "own":
                value = after(value, sums[at[0], tuple(range(chunks))][0])
            elif kind == "others":
                value = after(value, *sums[at[0], tuple(range(chunks))][1:])
            else:
                value = after(value, held[at[0]][kind])
        return value

    for kind, *step in steps:
        if kind == "move":
            name, h, ties = step
            sent, pairs = moves[name]
            held[h][name] = lax.ppermute(tied(held[h][sent], ties), "row", pairs)
        elif kind == "multiply":
            j, group, ties = step
            operands = [held[h][w] for h in group for w in (slots[j - 1][0] if j else ["own"])]
            operands[0] = tied(operands[0], ties)
            sums[j, group] = multiply(j, operands, group)
        else:
            j, groups = step
            result = gather(result, j, [x for group in groups for x in sums[j, group]])
    return result


def after(value, *others):
    return lax.optimization_barrier((value, *others))[0]


def solution(mesh):
    return jax.shard_map(
        functools.partial(on_device, mesh.shape["row"], mesh.shape["col"]),
        mesh=mesh,
        in_specs=(P(("col", "row"), None), P("row", "col"), P("row", "col"), P("col", None)),
        out_specs=P("col", "row"),
        check_vma=False,
    )
```

```python
import functools

import jax
import jax.numpy as jnp
import numpy as np
from jax import lax
from jax.experimental import pallas as pl
from jax.experimental.pallas import tpu as pltpu
from jax.sharding import PartitionSpec as P

TILE = 128
LANES = 128
CHUNKS = 2
MIB = 1 << 20


def row_plan(rows, chunks):
    moves, slots, steps = {}, [], []
    everything = tuple(range(chunks))
    if rows == 4 and chunks == 2:
        middle, outward = [(1, 2), (2, 1)], [(1, 0), (2, 3)]
        moves = {
            "pair": ("own", [(0, 1), (1, 0), (2, 3), (3, 2)]),
            "cross": ("own", middle),
            "far": ("cross", outward),
            "cross2": ("pair", middle),
            "far2": ("cross2", outward),
        }
        slots = [
            (["pair"], [0, 0, 0, 0], [1, 0, 3, 2]),
            (["far", "cross"], [0, 1, 1, 0], [2, 2, 1, 1]),
            (["far2", "cross2"], [0, 1, 1, 0], [3, 3, 0, 0]),
        ]
        steps = [
            ("move", "cross", 0, ()),
            ("move", "pair", 0, ()),
            ("multiply", 0, everything, ()),
            ("move", "cross", 1, (("own", 0),)),
            ("move", "pair", 1, (("own", 0),)),
            ("move", "far", 0, ()),
            ("multiply", 1, everything, (("far", 0),)),
            ("move", "cross2", 0, (("cross", 1),)),
            ("move", "far", 1, (("own", 1),)),
            ("move", "cross2", 1, (("cross2", 0),)),
            ("move", "far2", 0, (("own", 0),)),
            ("multiply", 2, everything, ()),
            ("move", "far2", 1, (("own", 2), ("others", 0), ("others", 1))),
            ("multiply", 3, everything, ()),
            ("add", 0, (everything,)),
            ("add", 1, (everything,)),
            ("add", 2, (everything,)),
            ("add", 3, (everything,)),
        ]
        return moves, slots, steps
    order = [[] for _ in range(rows)]
    for d in range(1, rows):
        low, high = f"low{d}", f"high{d}"
        moves[high] = (f"high{d - 1}" if d > 1 else "own", [(i + 1, i) for i in range(rows - d)])
        moves[low] = (f"low{d - 1}" if d > 1 else "own", [(i, i + 1) for i in range(d - 1, rows - 1)])
        for z in range(rows):
            order[z] += [(high, z + d)] * (z + d < rows) + [(low, z - d)] * (z >= d)
        steps += [("move", name, h, ()) for name in (high, low) for h in everything]
    for j in range(rows - 1):
        names = sorted({order[z][j][0] for z in range(rows)})
        slots.append((names, [names.index(order[z][j][0]) for z in range(rows)], [order[z][j][1] for z in range(rows)]))
    steps += [("multiply", j, everything, ()) for j in range(rows)] + [("add", j, (everything,)) for j in range(rows)]
    return moves, slots, steps


def split_amps(tiles, amps, *outs, chips, starts, width):
    chip, tile_row = lax.axis_index("col") // 2, lax.axis_index("row") * amps.shape[0] // TILE
    per = width // TILE
    for d in range(chips):
        there = chip ^ d
        for t in range(per):
            column = pl.multiple_of(there * width + t * TILE, TILE)
            kept = tiles[tile_row, there * per + t] != 0
            block = amps[:, pl.ds(column, TILE)]
            block = jnp.where(kept, block, jnp.zeros_like(block))
            for h in range(len(starts) - 1):
                outs[h * chips + d][:, t * TILE : (t + 1) * TILE] = block[starts[h] : starts[h + 1]]


def masked(block, tiles, first):
    rows = []
    for r in range(block.shape[0] // TILE):
        row = []
        for t in range(block.shape[1] // TILE):
            tile = block[r * TILE : (r + 1) * TILE, t * TILE : (t + 1) * TILE]
            row.append(jnp.where(tiles[first + r, t] != 0, tile, jnp.zeros_like(tile)))
        rows.append(jnp.concatenate(row, axis=1))
    return jnp.concatenate(rows, axis=0)


def first_sums(info, our_tiles, their_tiles, piece, *refs, **kw):
    n = kw["n_pieces"] - 1
    more, (ours, theirs), outs = refs[:n], refs[n : n + 2], refs[n + 2 :]
    our_kept, their_kept = outs[-4:-2]
    first = pl.program_id(0) * (ours.shape[0] // TILE)
    our_kept[...] = masked(ours[...], our_tiles, first)
    their_kept[...] = masked(theirs[...], their_tiles, first)
    partial_sums(info, piece, *more, our_kept, their_kept, *outs[:-4], *outs[-2:], **kw)


def partial_sums(info, *refs, n_pieces, n_choices, which, chips, tn):
    pieces = refs[: n_pieces * n_choices]
    ours, theirs = refs[n_pieces * n_choices : n_pieces * n_choices + 2]
    outs = refs[n_pieces * n_choices + 2 : -2]
    left, total = refs[-2:]
    step = pl.program_id(0)
    rows = [pieces[p * n_choices].shape[0] for p in range(n_pieces)]
    at = [sum(rows[:p]) for p in range(n_pieces)]

    @pl.when(step == 0)
    def _():
        for p in range(n_pieces):
            for c in range(n_choices):

                @pl.when((info[which] == c) if n_choices > 1 else True)
                def _():
                    left[at[p] : at[p] + rows[p]] = pieces[p * n_choices + c][...]

    half = ours.shape[1]
    core = info[1]
    mine = pl.multiple_of(core * half, half)
    other = pl.multiple_of((1 - core) * half, half)
    dims = (((1,), (1,)), ((), ()))
    sums = lax.dot_general(left[:, pl.ds(mine, half)], ours[...], dims, preferred_element_type=jnp.float32)
    sums += lax.dot_general(left[:, pl.ds(other, half)], theirs[...], dims, preferred_element_type=jnp.float32)
    total[:, pl.ds(pl.multiple_of(step * tn, tn), tn)] = sums

    @pl.when(step == pl.num_programs(0) - 1)
    def _():
        for p in range(n_pieces):
            one = rows[p] // chips
            there = slice(at[p] // chips, at[p] // chips + one)
            for d in range(chips):
                block = total[at[p] + d * one : at[p] + (d + 1) * one]
                if d == 0:
                    outs[0][there] = block
                else:
                    encode(block, outs[d].at[there])


def encode(block, out):
    width = block.shape[1]
    top = jnp.max(jnp.abs(block), axis=1, keepdims=True)
    power = jnp.ceil(jnp.log2(jnp.maximum(top, 2.0**-100)) + 0.01)
    out[:, :width] = jnp.round(block * (jnp.exp2(14.0 - power) * 1.98)).astype(jnp.int32).astype(jnp.int16)
    out[:, width:] = jnp.broadcast_to(power, (block.shape[0], LANES)).astype(jnp.int32).astype(jnp.int16)


def decode(coded, width):
    power = coded[:, width : width + 1].astype(jnp.int32).astype(jnp.float32)
    return coded[:, :width].astype(jnp.int32).astype(jnp.float32) * (jnp.exp2(power - 14.0) * (1.0 / 1.98))


def add_up(info, *refs, chips):
    sets, out, at = refs[:-1], refs[-1], 0
    for g in range(0, len(sets), chips):
        total = sets[g][...]
        for d in range(1, chips):
            total += decode(sets[g + d][...], total.shape[1])
        out[at : at + total.shape[0]] = total
        at += total.shape[0]


def call(body, name, grid, in_specs, out_specs, out_shape, scalars, args, scratch=(), flops=0, moved=0, aliases=None):
    return pl.pallas_call(
        body,
        out_shape=out_shape,
        grid_spec=pltpu.PrefetchScalarGridSpec(
            num_scalar_prefetch=len(scalars), grid=grid, in_specs=in_specs, out_specs=out_specs, scratch_shapes=list(scratch)
        ),
        compiler_params=pltpu.CompilerParams(vmem_limit_bytes=24 * MIB),
        cost_estimate=pl.CostEstimate(flops=flops, bytes_accessed=0, transcendentals=0),
        input_output_aliases=aliases or {},
        name=name,
    )(*scalars, *args)


def whole(shape):
    return pl.BlockSpec(shape, lambda *_: (0,) * len(shape))


def on_device(n_row, n_col, amplitudes, integrals, integral_tiles, amplitude_tiles):
    chips, chunks = n_col // 2, CHUNKS
    m, cds = amplitudes.shape
    width = cds // chips
    starts = [0, 3 * m // 4, m]
    rows_of = [b - a for a, b in zip(starts, starts[1:])]
    nab, half = integrals.shape

    moves, slots, steps = row_plan(n_row, chunks)
    table = []
    for z in range(n_row):
        picks = [0] + [slot[1][z] for slot in slots]
        sources = [z] + [slot[2][z] for slot in slots]
        for c in range(n_col):
            table.append([c // 2, c % 2, z * m // TILE, *picks, *sources])
    table = np.array(table, np.int32)
    here = lax.axis_index("row") * n_col + lax.axis_index("col")
    info = lax.dynamic_index_in_dim(jnp.asarray(table), here, 0, keepdims=False)
    pick_at, source_at = 3, 3 + n_row

    def over(d):
        return [(i, i ^ (2 * d)) for i in range(n_col)]

    swap = [(i, i ^ 1) for i in range(n_col)]
    theirs = lax.ppermute(integrals, "col", swap)
    their_tiles = lax.ppermute(integral_tiles, "col", swap)
    kept = []

    parts = call(
        functools.partial(split_amps, chips=chips, starts=starts, width=width),
        "split_amps",
        (1,),
        [whole(amplitudes.shape)],
        [whole((rows, width)) for rows in rows_of for _ in range(chips)],
        [jax.ShapeDtypeStruct((rows, width), jnp.bfloat16) for rows in rows_of for _ in range(chips)],
        (amplitude_tiles,),
        (amplitudes,),
        moved=4 * m * cds,
    )
    pieces = []
    for h in range(chunks):
        got = [parts[h * chips]]
        for d in range(1, chips):
            part = parts[h * chips + d]
            got.append(lax.ppermute(after(part, their_tiles) if h else part, "col", over(d)))
        pieces.append(jnp.concatenate(got, axis=0))

    tn = min(1024, nab)

    def multiply(j, operands, group):
        wanted = ["own"] if j == 0 else slots[j - 1][0]
        many = sum(rows_of[h] for h in group)
        block = pl.BlockSpec((tn, half), lambda i, *_: (i, 0))
        out = [((many, nab), jnp.float32)] + [((many, nab + LANES), jnp.int16)] * (chips - 1)
        outs = call(
            functools.partial(
                partial_sums if j else first_sums,
                n_pieces=len(group),
                n_choices=len(wanted),
                which=pick_at + j,
                chips=chips,
                tn=tn,
            ),
            "partial_sums" if j else "first_sums",
            (nab // tn,),
            [whole(x.shape) for x in operands] + [block] * 2,
            [whole(shape) for shape, _ in out] + ([] if j else [block] * 2),
            [jax.ShapeDtypeStruct(*x) for x in out] + ([] if j else [jax.ShapeDtypeStruct((nab, half), jnp.bfloat16)] * 2),
            (info,) if j else (info, integral_tiles, their_tiles),
            (*operands, *(kept if j else (pltpu.with_memory_space_constraint(integrals, pltpu.HBM), theirs))),
            scratch=[
                pltpu.VMEM((chips * many, width), jnp.bfloat16),
                pltpu.VMEM((chips * many, nab), jnp.float32),
            ],
        )
        if not j:
            kept.extend(outs[-2:])
        return [outs[0]] + [lax.ppermute(outs[d], "col", over(d)) for d in range(1, chips)]

    def gather(result, j, sums):
        def place(i, info):
            return (info[source_at + j], 0)

        body = functools.partial(add_up, chips=chips)
        specs = [whole(x.shape) for x in sums]
        args, aliases = tuple(sums), {}
        if result is not None:
            body = functools.partial(lambda f, info, base, *refs: f(info, *refs), body)
            specs = [pl.BlockSpec(memory_space=pl.ANY)] + specs
            args, aliases = (result, *args), {1: 0}
        return call(
            body,
            "add_up",
            (1,),
            specs,
            pl.BlockSpec((m, nab), place),
            jax.ShapeDtypeStruct((n_row * m, nab), jnp.float32),
            (info,),
            args,
            aliases=aliases,
            moved=16 * m * nab,
        )

    held = [{"own": pieces[h]} for h in range(chunks)]
    sums, result = {}, None

    def tied(value, ties):
        nonlocal result
        for kind, *at in ties:
            if kind == "result":
                value, result = lax.optimization_barrier((value, result))
            elif kind == "own":
                value = after(value, sums[at[0], tuple(range(chunks))][0])
            elif kind == "others":
                value = after(value, *sums[at[0], tuple(range(chunks))][1:])
            else:
                value = after(value, held[at[0]][kind])
        return value

    for kind, *step in steps:
        if kind == "move":
            name, h, ties = step
            sent, pairs = moves[name]
            held[h][name] = lax.ppermute(tied(held[h][sent], ties), "row", pairs)
        elif kind == "multiply":
            j, group, ties = step
            operands = [held[h][w] for h in group for w in (slots[j - 1][0] if j else ["own"])]
            operands[0] = tied(operands[0], ties)
            sums[j, group] = multiply(j, operands, group)
        else:
            j, groups = step
            result = gather(result, j, [x for group in groups for x in sums[j, group]])
    return result


def after(value, *others):
    return lax.optimization_barrier((value, *others))[0]


def solution(mesh):
    return jax.shard_map(
        functools.partial(on_device, mesh.shape["row"], mesh.shape["col"]),
        mesh=mesh,
        in_specs=(P(("col", "row"), None), P("row", "col"), P("row", "col"), P("col", None)),
        out_specs=P("col", "row"),
        check_vma=False,
    )
```
